32 devices in a mesh: fsdp: 16 (over z, y, core), seq: 2 (over x).
Axes of the slice: x: 2, y: 2, z: 4, core: 2. Of those that a mesh axis runs over, the one named last changes fastest.
Arguments:
- hidden: bfloat16 [32, 1024, 768], P('fsdp', 'seq'), may hold values from -6 to 6
- segments: int32 [32, 1024], P('fsdp'), may hold values from 0 to 7, never falling along the last dimension, each value on 1 to 512 neighbouring positions
- block_perm: int32 [12, 2], replicated, may hold values from 0 to 1, each once within a row
- query_weight: bfloat16 [768, 768], P('fsdp'), may hold values from -0.21875 to 0.21875
- query_bias: bfloat16 [768], P('fsdp'), may hold values from -3 to 3
- key_weight: bfloat16 [768, 768], P('fsdp'), may hold values from -0.21875 to 0.21875
- value_weight: bfloat16 [768, 768], P('fsdp'), may hold values from -0.21875 to 0.21875
- value_bias: bfloat16 [768], P('fsdp'), may hold values from -3 to 3
- output_weight: bfloat16 [768, 768], P('fsdp'), may hold values from -0.875 to 0.875
- output_bias: bfloat16 [768], P('fsdp'), may hold values from -3 to 3
- first_gain: bfloat16 [768], P('fsdp'), may hold values from 0.5 to 1.5
- first_shift: bfloat16 [768], P('fsdp'), may hold values from -3 to 3
- inner_weight: bfloat16 [768, 3072], P('fsdp'), may hold values from -0.21875 to 0.21875
- inner_bias: bfloat16 [3072], P('fsdp'), may hold values from -3 to 3
- outer_weight: bfloat16 [3072, 768], P('fsdp'), may hold values from -0.109375 to 0.109375
- outer_bias: bfloat16 [768], P('fsdp'), may hold values from -3 to 3
- second_gain: bfloat16 [768], P('fsdp'), may hold values from 0.5 to 1.5
- second_shift: bfloat16 [768], P('fsdp'), may hold values from -3 to 3
- cotangent: bfloat16 [32, 1024, 768], P('fsdp', 'seq'), may hold values from -6 to 6
Outputs:
- layer_out: bfloat16 [32, 1024, 768], P('fsdp', 'seq')
- hidden_grad: bfloat16 [32, 1024, 768], P('fsdp', 'seq')
- query_weight_grad: float32 [768, 768], P('fsdp')
- query_bias_grad: float32 [768], P('fsdp')
- key_weight_grad: float32 [768, 768], P('fsdp')
- value_weight_grad: float32 [768, 768], P('fsdp')
- value_bias_grad: float32 [768], P('fsdp')
- output_weight_grad: float32 [768, 768], P('fsdp')
- output_bias_grad: float32 [768], P('fsdp')
- first_gain_grad: float32 [768], P('fsdp')
- first_shift_grad: float32 [768], P('fsdp')
- inner_weight_grad: float32 [768, 3072], P('fsdp')
- inner_bias_grad: float32 [3072], P('fsdp')
- outer_weight_grad: float32 [3072, 768], P('fsdp')
- outer_bias_grad: float32 [768], P('fsdp')
- second_gain_grad: float32 [768], P('fsdp')
- second_shift_grad: float32 [768], P('fsdp')
The draws below stay inside these ranges and needn't reach their ends.
Inputs may be any that keep to these rules, and one draw needn't show every extreme that they name: `segments`: segment numbers never fall along a sequence; each document spans at most 512 tokens and one spans exactly that many. `block_perm`: each row names each of the 2 blocks once.
All inputs are finite; a program needn't handle non-finite values.
Results may differ from the reference program's by a relative error of at most 0.015.
Values may be sent and summed in bfloat16 or wider, within the bound.
No kernel may reach another device: no remote copies, remote signals or barrier semaphores. Data moves between devices by JAX's collectives and lax.ppermute only.
A program may use at most 192 MiB of HBM per device.

```python
import math
import jax
import jax.numpy as jnp
import numpy as np
from jax import lax

D = 768
H = 12
HD = 64
FF = 3072
L = 1024
NB = 2
BLK = 512
SEQS = 32


def block_levels(stream_key, dims, cuts, low, high):
    def one(position, shards_of):
        heights = jax.random.uniform(jax.random.fold_in(jax.random.fold_in(stream_key, 6), position), (shards_of,), jnp.float32, low / len(cuts), high / len(cuts))
        return jnp.repeat(jnp.exp(heights), dims[position] // shards_of).reshape((-1,) + (1,) * (len(dims) - position - 1))

    factor_of = one(*cuts[0])
    for cut in cuts[1:]:
        factor_of = factor_of * one(*cut)
    return factor_of


def split_up(count, total, limit, skew):
    loads = [(1 << 20) // math.isqrt(standing ** skew) + 1 for standing in range(2, count + 1)]
    rest, counts = total - limit - (count - 1), [1] * (count - 1)
    while rest > 0:
        movable = [i for i in range(count - 1) if counts[i] < limit]
        whole, budget = sum([loads[i] for i in movable]), rest
        for i in movable:
            addition = min(limit - counts[i], max(1, budget * loads[i] // whole), rest)
            counts[i] = counts[i] + addition
            rest = rest - addition
    return np.array([limit] + counts)


def uneven_parts(stream_key, amount, total, most, skew):
    if amount == 2:
        one = jax.random.randint(stream_key, (), max(1, total - most), min(most, total - 1) + 1)
        return jnp.stack([one, total - one])
    tallies = jnp.asarray(split_up(amount, total, most, skew), jnp.int32)
    pairs = (amount - 1) // 2
    giver, receiver = tallies[1:1 + 2 * pairs:2], tallies[2:2 + 2 * pairs:2]
    margin = jnp.minimum(giver - 1, most - receiver)
    shifted = jax.random.randint(jax.random.fold_in(stream_key, 1), (pairs,), 0, 1 << 20) % (margin + 1)
    tallies = tallies.at[1:1 + 2 * pairs:2].set(giver - shifted).at[2:2 + 2 * pairs:2].set(receiver + shifted)
    return tallies[jax.random.permutation(jax.random.fold_in(stream_key, 2), amount)]


def noise(key, extent, deviation, most, cuts=(), kind=jnp.bfloat16):
    factor_of = block_levels(key, extent, cuts, -0.22, 0.18) if cuts else 1.0
    drawn = jax.random.normal(key, extent, jnp.float32) * deviation * factor_of
    return jnp.minimum(jnp.maximum(drawn, -most), most).astype(kind)


def setup_inputs(seed: int = 0) -> dict:
    streams_of = jax.random.split(jax.random.key(seed), 20)
    return {
        "hidden": noise(streams_of[0], (SEQS, L, D), 1.0, 6.0, ((0, 16), (1, 2))),
        "segments": jax.vmap(lambda own: jnp.searchsorted(jnp.cumsum(uneven_parts(own, 8, L, L // 2, 0)), jnp.arange(L), side="right"))(jax.random.split(streams_of[1], SEQS)).reshape((SEQS, L)).astype(jnp.int32),
        "block_perm": jax.vmap(lambda own: jax.random.permutation(own, NB))(jax.random.split(streams_of[2], H)).reshape((H, NB)).astype(jnp.int32),
        "query_weight": noise(streams_of[3], (D, D), D ** -0.5, 0.21875, ((0, 16),)),
        "query_bias": noise(streams_of[4], (D,), 0.5, 3.0, ((0, 16),)),
        "key_weight": noise(streams_of[5], (D, D), D ** -0.5, 0.21875, ((0, 16),)),
        "value_weight": noise(streams_of[6], (D, D), D ** -0.5, 0.21875, ((0, 16),)),
        "value_bias": noise(streams_of[7], (D,), 0.5, 3.0, ((0, 16),)),
        "output_weight": noise(streams_of[8], (D, D), (D // 16) ** -0.5, 0.875, ((0, 16),)),
        "output_bias": noise(streams_of[9], (D,), 0.5, 3.0, ((0, 16),)),
        "first_gain": jnp.clip(1.0 + 0.1 * jax.random.normal(streams_of[10], (D,), jnp.float32), 0.5, 1.5).astype(jnp.bfloat16),
        "first_shift": noise(streams_of[11], (D,), 0.5, 3.0, ((0, 16),)),
        "inner_weight": noise(streams_of[12], (D, FF), D ** -0.5, 0.21875, ((0, 16),)),
        "inner_bias": noise(streams_of[13], (FF,), 0.5, 3.0, ((0, 16),)),
        "outer_weight": noise(streams_of[14], (FF, D), FF ** -0.5, 0.109375, ((0, 16),)),
        "outer_bias": noise(streams_of[15], (D,), 0.5, 3.0, ((0, 16),)),
        "second_gain": jnp.clip(1.0 + 0.1 * jax.random.normal(streams_of[16], (D,), jnp.float32), 0.5, 1.5).astype(jnp.bfloat16),
        "second_shift": noise(streams_of[17], (D,), 0.5, 3.0, ((0, 16),)),
        "cotangent": noise(streams_of[18], (SEQS, L, D), 1.0, 6.0, ((0, 16), (1, 2))),
    }


HIGH = lax.Precision.HIGHEST
EPSILON = 1e-05

@jax.custom_vjp
def low(v):
    return lax.optimization_barrier(v.astype(jnp.bfloat16)).astype(jnp.float32)

@jax.custom_vjp
def low_back(v):
    return v

def low_keep(v):
    return (low(v), None)

def low_pass(kept, grad):
    return (grad,)

def back_keep(v):
    return (v, None)

def back_low(kept, grad):
    return (low(grad),)
low.defvjp(low_keep, low_pass)
low_back.defvjp(back_keep, back_low)

def dense(left, right):
    return jnp.dot(left, right, precision=HIGH, preferred_element_type=jnp.float32)

def norm_rows(values, gain, shift):
    average = lax.optimization_barrier(jnp.mean(values, axis=-1, keepdims=True))
    centered = values - average
    spread = lax.optimization_barrier(jnp.mean(centered * centered, axis=-1, keepdims=True))
    return centered * lax.rsqrt(spread + EPSILON) * gain + shift

def attend(query, keys, values, segment_row, block_perm):
    scale = HD ** (-0.5)
    shaped = (NB, BLK, H, HD)
    query_split = query.reshape(shaped)
    keys_split = keys.reshape(shaped).transpose(2, 0, 1, 3)
    values_split = values.reshape(shaped).transpose(2, 0, 1, 3)
    segment_split = segment_row.reshape(NB, BLK)
    mirror = jnp.arange(BLK, dtype=jnp.int32)[:, None] == jnp.arange(BLK, dtype=jnp.int32)[None, :]
    pieces = []
    for block in range(NB):
        target = block_perm[:, block].astype(jnp.int32)
        chosen_keys = jnp.take_along_axis(keys_split, target[:, None, None, None], axis=1)[:, 0]
        chosen_values = jnp.take_along_axis(values_split, target[:, None, None, None], axis=1)[:, 0]
        key_segments = segment_split[target]
        scores = jnp.einsum('qhd,hkd->hqk', query_split[block], chosen_keys, precision=HIGH) * scale
        scores = low_back(scores)
        allowed = (segment_split[block][None, :, None] == key_segments[:, None, :]) | mirror[None]
        probs = jax.nn.softmax(jnp.where(allowed, scores, -1e+30), axis=-1)
        probs = low(probs)
        pieces.append(jnp.einsum('hqk,hkd->qhd', probs, chosen_values, precision=HIGH))
    return jnp.concatenate(pieces, axis=0)

def forward(rows, weights, segments, block_perm):
    query_weight, query_bias, key_weight, value_weight, value_bias, output_weight, output_bias, first_gain, first_shift, inner_weight, inner_bias, outer_weight, outer_bias, second_gain, second_shift = weights
    query = low_back(low(dense(rows, query_weight) + query_bias))
    keys = low_back(low(dense(rows, key_weight)))
    values = low_back(low(dense(rows, value_weight) + value_bias))
    shaped = (SEQS, L, H, HD)
    context = lax.map(lambda items: jax.checkpoint(attend)(items[0], items[1], items[2], items[3], block_perm), (query.reshape(shaped), keys.reshape(shaped), values.reshape(shaped), segments))
    context = low_back(low(context.reshape(SEQS * L, D)))
    attn_out = low_back(dense(context, output_weight) + output_bias)
    first = rows + attn_out
    normed = norm_rows(first, first_gain, first_shift)
    inner = low_back(dense(low(normed), inner_weight) + inner_bias)
    active = low(jax.nn.gelu(inner, approximate=False))
    outer = low_back(dense(active, outer_weight) + outer_bias)
    second = normed + outer
    return norm_rows(second, second_gain, second_shift)

def reference(hidden, segments, block_perm, query_weight, query_bias, key_weight, value_weight, value_bias, output_weight, output_bias, first_gain, first_shift, inner_weight, inner_bias, outer_weight, outer_bias, second_gain, second_shift, cotangent):
    weights = tuple((w.astype(jnp.float32) for w in (query_weight, query_bias, key_weight, value_weight, value_bias, output_weight, output_bias, first_gain, first_shift, inner_weight, inner_bias, outer_weight, outer_bias, second_gain, second_shift)))
    rows = hidden.astype(jnp.float32).reshape(SEQS * L, D)
    result, pullback = jax.vjp(lambda inputs, params: forward(inputs, params, segments, block_perm), rows, weights)
    rows_grad, grads = pullback(cotangent.astype(jnp.float32).reshape(SEQS * L, D))
    return (result.reshape(SEQS, L, D).astype(jnp.bfloat16), rows_grad.reshape(SEQS, L, D).astype(jnp.bfloat16), grads[0], grads[1], grads[2], grads[3], grads[4], grads[5], grads[6], grads[7], grads[8], grads[9], grads[10], grads[11], grads[12], grads[13], grads[14])
```

```python
import jax
import jax.numpy as jnp
from jax import lax
from jax.sharding import PartitionSpec as P

H = 12
HD = 64


EPSILON = 1e-05


def shortened(array):
    return jax.tree.map(lambda a: a.astype(jnp.bfloat16) if a.dtype == jnp.float32 else a, array)


def norm_core(values, gain):
    average = jnp.mean(values, axis=-1, keepdims=True)
    centered = values - average
    spread = jnp.mean(centered * centered, axis=-1, keepdims=True)
    return centered * lax.rsqrt(spread + EPSILON) * gain


def exact_gelu(values):
    return jax.nn.gelu(values, approximate=False)


def matmul(left, right):
    return jnp.dot(left, right, preferred_element_type=jnp.float32)


def times_transposed(left, right):
    return lax.dot_general(
        left, right, (((1,), (1,)), ((), ())), preferred_element_type=jnp.float32
    )


def transposed_times(left, right):
    return lax.dot_general(
        left, right, (((0,), (0,)), ((), ())), preferred_element_type=jnp.float32
    )


def column_sum(values):
    return jnp.sum(values.astype(jnp.float32), axis=0)


def select_blocks(blocked, target):
    return jnp.take_along_axis(blocked, target[:, None, None, None], axis=1)[:, 0]


def block_scores(query_block, chosen_keys, query_segments, key_segments, scale):
    scores = (
        jnp.einsum("qhd,hkd->hqk", query_block, chosen_keys, preferred_element_type=jnp.float32)
        * scale
    )
    same_doc = query_segments[None, :, None] == key_segments[:, None, :]
    mirror = lax.broadcasted_iota(jnp.int32, scores.shape, 1) == lax.broadcasted_iota(
        jnp.int32, scores.shape, 2
    )
    return jnp.where(same_doc | mirror, scores, -1e30)


def split_layout(query_all, keys_all, values_all, segment_row, perm_local, head_dim):
    length, width = query_all.shape
    heads = width // head_dim
    block_count = perm_local.shape[1]
    block_rows = length // block_count
    shaped = (block_count, block_rows, heads, head_dim)
    query_split = query_all.reshape(shaped)
    keys_split = keys_all.reshape(shaped).transpose(2, 0, 1, 3)
    values_split = values_all.reshape(shaped).transpose(2, 0, 1, 3)
    segment_split = segment_row.reshape(block_count, block_rows)
    return (query_split, keys_split, values_split, segment_split, shaped)


def attend_forward(query_all, keys_all, values_all, segment_row, perm_local, head_dim):
    length, width = query_all.shape
    query_split, keys_split, values_split, segment_split, shaped = split_layout(
        query_all, keys_all, values_all, segment_row, perm_local, head_dim
    )
    scale = head_dim ** (-0.5)
    contexts = []
    log_totals = []
    for block in range(shaped[0]):
        target = perm_local[:, block]
        chosen_keys = select_blocks(keys_split, target)
        chosen_values = select_blocks(values_split, target)
        masked = block_scores(
            query_split[block], chosen_keys, segment_split[block], segment_split[target], scale
        )
        row_max = jnp.max(masked, axis=-1, keepdims=True)
        lifted = jnp.exp(masked - row_max)
        total = jnp.sum(lifted, axis=-1, keepdims=True)
        probs = (lifted / total).astype(jnp.bfloat16)
        piece = jnp.einsum("hqk,hkd->qhd", probs, chosen_values, preferred_element_type=jnp.float32)
        contexts.append(piece.astype(jnp.bfloat16))
        log_totals.append(row_max + jnp.log(total))
    return (jnp.concatenate(contexts, axis=0).reshape(length, width), jnp.stack(log_totals))


def attend_backward(
    query_all, keys_all, values_all, slope_all, segment_row, perm_local, log_totals, head_dim
):
    length, width = query_all.shape
    query_split, keys_split, values_split, segment_split, shaped = split_layout(
        query_all, keys_all, values_all, segment_row, perm_local, head_dim
    )
    block_count, block_rows, heads = (shaped[0], shaped[1], shaped[2])
    slope_split = slope_all.reshape(shaped)
    scale = head_dim ** (-0.5)
    key_slots = jnp.zeros((heads, block_count, block_rows, head_dim), jnp.float32)
    value_slots = jnp.zeros((heads, block_count, block_rows, head_dim), jnp.float32)
    block_ids = jnp.arange(block_count, dtype=jnp.int32)
    query_slopes = []
    for block in range(block_count):
        target = perm_local[:, block]
        chosen_keys = select_blocks(keys_split, target)
        chosen_values = select_blocks(values_split, target)
        masked = block_scores(
            query_split[block], chosen_keys, segment_split[block], segment_split[target], scale
        )
        probs = jnp.exp(masked - log_totals[block])
        slope_probs = jnp.einsum(
            "qhd,hkd->hqk", slope_split[block], chosen_values, preferred_element_type=jnp.float32
        )
        row_dot = jnp.sum(probs * slope_probs, axis=-1, keepdims=True)
        slope_scores = (probs * (slope_probs - row_dot)).astype(jnp.bfloat16)
        query_part = (
            jnp.einsum(
                "hqk,hkd->qhd", slope_scores, chosen_keys, preferred_element_type=jnp.float32
            )
            * scale
        )
        query_slopes.append(query_part.astype(jnp.bfloat16))
        key_part = (
            jnp.einsum(
                "hqk,qhd->hkd", slope_scores, query_split[block], preferred_element_type=jnp.float32
            )
            * scale
        )
        value_part = jnp.einsum(
            "hqk,qhd->hkd",
            probs.astype(jnp.bfloat16),
            slope_split[block],
            preferred_element_type=jnp.float32,
        )
        hit = (target[:, None] == block_ids[None, :])[:, :, None, None]
        key_slots = jnp.where(hit, key_part[:, None], key_slots)
        value_slots = jnp.where(hit, value_part[:, None], value_slots)
    slope_query = jnp.concatenate(query_slopes, axis=0).reshape(length, width)
    slope_keys = key_slots.transpose(1, 2, 0, 3).reshape(length, width).astype(jnp.bfloat16)
    slope_values = value_slots.transpose(1, 2, 0, 3).reshape(length, width).astype(jnp.bfloat16)
    return (slope_query, slope_keys, slope_values)


def on_device_general(
    hidden,
    segments,
    block_perm,
    query_weight,
    query_bias,
    key_weight,
    value_weight,
    value_bias,
    output_weight,
    output_bias,
    first_gain,
    first_shift,
    inner_weight,
    inner_bias,
    outer_weight,
    outer_bias,
    second_gain,
    second_shift,
    cotangent,
):
    micro = hidden.shape[0]
    heads_here = H // lax.axis_size("seq")
    perm_local = lax.dynamic_slice_in_dim(
        block_perm, lax.axis_index("seq") * heads_here, heads_here, 0
    )
    shards = (
        query_weight,
        query_bias,
        key_weight,
        value_weight,
        value_bias,
        output_weight,
        output_bias,
        first_gain,
        first_shift,
        inner_weight,
        inner_bias,
        outer_weight,
        outer_bias,
        second_gain,
        second_shift,
    )
    matrices = (
        query_weight,
        key_weight,
        value_weight,
        output_weight,
        inner_weight,
        outer_weight,
        first_gain,
        second_gain,
    )
    sums = tuple(
        (
            jnp.zeros((piece.shape[0] * lax.axis_size("fsdp"),) + piece.shape[1:], jnp.float32)
            for piece in shards
        )
    )
    f32 = jnp.float32
    bf16 = jnp.bfloat16

    def one_batch(index, carry):
        layer_out, hidden_grad, totals = carry
        rows = lax.dynamic_index_in_dim(hidden, index, 0, keepdims=False)
        segment_row = lax.dynamic_index_in_dim(segments, index, 0, keepdims=False)
        grad_out = lax.dynamic_index_in_dim(cotangent, index, 0, keepdims=False).astype(f32)
        ahead = (
            lax.all_gather(shards[0], "fsdp", axis=0, tiled=True),
            lax.all_gather(shards[1], "fsdp", axis=0, tiled=True),
            lax.all_gather(shards[2], "fsdp", axis=0, tiled=True),
            lax.all_gather(shards[3], "fsdp", axis=0, tiled=True),
            lax.all_gather(shards[4], "fsdp", axis=0, tiled=True),
            lax.all_gather(shards[5], "fsdp", axis=0, tiled=True),
            lax.all_gather(shards[6], "fsdp", axis=0, tiled=True),
            lax.all_gather(shards[7], "fsdp", axis=0, tiled=True),
            lax.all_gather(shards[8], "fsdp", axis=0, tiled=True),
            lax.all_gather(shards[9], "fsdp", axis=0, tiled=True),
            lax.all_gather(shards[10], "fsdp", axis=0, tiled=True),
            lax.all_gather(shards[11], "fsdp", axis=0, tiled=True),
            lax.all_gather(shards[12], "fsdp", axis=0, tiled=True),
            lax.all_gather(shards[13], "fsdp", axis=0, tiled=True),
            lax.all_gather(shards[14], "fsdp", axis=0, tiled=True),
        )
        (
            whole_query,
            query_shift,
            whole_key,
            whole_value,
            value_shift,
            whole_output,
            output_shift,
            gain_one,
            shift_one,
            whole_inner,
            inner_shift,
            whole_outer,
            outer_shift,
            gain_two,
            shift_two,
        ) = ahead
        query = (matmul(rows, whole_query) + query_shift.astype(f32)).astype(bf16)
        keys = matmul(rows, whole_key).astype(bf16)
        values = (matmul(rows, whole_value) + value_shift.astype(f32)).astype(bf16)
        query_all, keys_all, values_all = (
            lax.all_to_all(query, "seq", split_axis=1, concat_axis=0, tiled=True),
            lax.all_to_all(keys, "seq", split_axis=1, concat_axis=0, tiled=True),
            lax.all_to_all(values, "seq", split_axis=1, concat_axis=0, tiled=True),
        )
        context, log_totals = attend_forward(
            query_all, keys_all, values_all, segment_row, perm_local, HD
        )
        context_rows = lax.all_to_all(
            shortened(context), "seq", split_axis=0, concat_axis=1, tiled=True
        ).astype(context.dtype)
        first = rows.astype(f32) + (matmul(context_rows, whole_output) + output_shift.astype(f32))
        normed = norm_core(first, gain_one.astype(f32)) + shift_one.astype(f32)
        normed_low = normed.astype(bf16)
        inner = matmul(normed_low, whole_inner) + inner_shift.astype(f32)
        active = exact_gelu(inner).astype(bf16)
        second = normed + (matmul(active, whole_outer) + outer_shift.astype(f32))
        result = norm_core(second, gain_two.astype(f32)) + shift_two.astype(f32)
        behind = (
            lax.all_gather(matrices[0], "fsdp", axis=0, tiled=True),
            lax.all_gather(matrices[1], "fsdp", axis=0, tiled=True),
            lax.all_gather(matrices[2], "fsdp", axis=0, tiled=True),
            lax.all_gather(matrices[3], "fsdp", axis=0, tiled=True),
            lax.all_gather(matrices[4], "fsdp", axis=0, tiled=True),
            lax.all_gather(matrices[5], "fsdp", axis=0, tiled=True),
            lax.all_gather(matrices[6], "fsdp", axis=0, tiled=True),
            lax.all_gather(matrices[7], "fsdp", axis=0, tiled=True),
        )
        (
            back_query,
            back_key,
            back_value,
            back_output,
            back_inner,
            back_outer,
            back_gain_one,
            back_gain_two,
        ) = behind
        _, second_back = jax.vjp(norm_core, second, back_gain_two.astype(f32))
        slope_second, grad_gain_two = second_back(grad_out)
        grad_shift_two = jnp.sum(grad_out, axis=0)
        slope_outer = slope_second.astype(bf16)
        grad_outer_shift = column_sum(slope_outer)
        grad_outer = transposed_times(active, slope_outer)
        _, gelu_back = jax.vjp(exact_gelu, inner)
        slope_inner = gelu_back(times_transposed(slope_outer, back_outer))[0].astype(bf16)
        grad_inner_shift = column_sum(slope_inner)
        grad_inner = transposed_times(normed_low, slope_inner)
        slope_normed = slope_second + times_transposed(slope_inner, back_inner)
        _, first_back = jax.vjp(norm_core, first, back_gain_one.astype(f32))
        slope_first, grad_gain_one = first_back(slope_normed)
        grad_shift_one = jnp.sum(slope_normed, axis=0)
        slope_attn = slope_first.astype(bf16)
        grad_output_shift = column_sum(slope_attn)
        grad_output = transposed_times(context_rows, slope_attn)
        slope_context = times_transposed(slope_attn, back_output).astype(bf16)
        slope_context_all = lax.all_to_all(
            slope_context, "seq", split_axis=1, concat_axis=0, tiled=True
        )
        slope_query_all, slope_keys_all, slope_values_all = attend_backward(
            query_all,
            keys_all,
            values_all,
            slope_context_all,
            segment_row,
            perm_local,
            log_totals,
            HD,
        )
        slope_query, slope_keys, slope_values = (
            lax.all_to_all(
                shortened(slope_query_all), "seq", split_axis=0, concat_axis=1, tiled=True
            ).astype(slope_query_all.dtype),
            lax.all_to_all(slope_keys_all, "seq", split_axis=0, concat_axis=1, tiled=True),
            lax.all_to_all(slope_values_all, "seq", split_axis=0, concat_axis=1, tiled=True),
        )
        grad_query = transposed_times(rows, slope_query)
        grad_query_shift = column_sum(slope_query)
        grad_key = transposed_times(rows, slope_keys)
        grad_value = transposed_times(rows, slope_values)
        grad_value_shift = column_sum(slope_values)
        slope_rows = (
            slope_first
            + times_transposed(slope_query, back_query)
            + times_transposed(slope_keys, back_key)
            + times_transposed(slope_values, back_value)
        )
        grads = (
            grad_query,
            grad_query_shift,
            grad_key,
            grad_value,
            grad_value_shift,
            grad_output,
            grad_output_shift,
            grad_gain_one,
            grad_shift_one,
            grad_inner,
            grad_inner_shift,
            grad_outer,
            grad_outer_shift,
            grad_gain_two,
            grad_shift_two,
        )
        totals = jax.tree.map(lambda total, piece: total + piece, totals, grads)
        layer_out = lax.dynamic_update_index_in_dim(layer_out, result.astype(bf16), index, 0)
        hidden_grad = lax.dynamic_update_index_in_dim(
            hidden_grad, slope_rows.astype(bf16), index, 0
        )
        return (layer_out, hidden_grad, totals)

    start = (jnp.zeros(hidden.shape, bf16), jnp.zeros(hidden.shape, bf16), sums)
    layer_out, hidden_grad, sums = lax.fori_loop(0, micro, one_batch, start)
    owned = lax.psum_scatter(sums, "fsdp", scatter_dimension=0, tiled=True)
    sums = jax.tree.map(lambda part: part.astype(jnp.float32), lax.psum(shortened(owned), "seq"))
    return (layer_out, hidden_grad) + tuple(sums)


def attention_forward(query, keys, values, segment_row, block_perm):
    return attend_forward(query, keys, values, segment_row, block_perm, HD)


def attention_backward(query, keys, values, slope, segment_row, block_perm, log_totals):
    return attend_backward(
        query, keys, values, slope, segment_row, block_perm, log_totals, HD
    )


def to_whole_sequences(array):
    return lax.all_to_all(array, "seq", split_axis=0, concat_axis=1, tiled=True)


def to_token_shards(array):
    return lax.all_to_all(array, "seq", split_axis=1, concat_axis=0, tiled=True)


def sum_over_seq(array):
    if lax.axis_size("seq") == 2:
        return array + lax.ppermute(array, "seq", [(0, 1), (1, 0)])
    return lax.psum(array, "seq")


def on_device_whole(
    hidden,
    segments,
    block_perm,
    query_weight,
    query_bias,
    key_weight,
    value_weight,
    value_bias,
    output_weight,
    output_bias,
    first_gain,
    first_shift,
    inner_weight,
    inner_bias,
    outer_weight,
    outer_bias,
    second_gain,
    second_shift,
    cotangent,
):
    f32 = jnp.float32
    bf16 = jnp.bfloat16
    micro = hidden.shape[0]
    seqs = lax.axis_size("seq")
    owners = lax.axis_size("fsdp")
    each = micro // seqs
    part, width = query_weight.shape
    wide = inner_weight.shape[1]
    spans = wide // width
    small = (
        query_bias,
        value_bias,
        output_bias,
        first_gain,
        first_shift,
        outer_bias,
        second_gain,
        second_shift,
        inner_bias,
    )
    small_sizes = [piece.shape[0] for piece in small]
    small_count = sum(small_sizes)
    small_rows = -(-small_count // (16 * width)) * 16

    def small_block(pieces, lead):
        flat = jnp.concatenate(pieces, axis=-1)
        flat = jnp.pad(flat, [(0, 0)] * len(lead) + [(0, small_rows * width - small_count)])
        return flat.reshape(lead + (small_rows, width))

    early_pack = jnp.concatenate(
        [query_weight, key_weight, value_weight, small_block(small, ())], axis=0
    )
    late_pack = jnp.concatenate(
        [output_weight]
        + [inner_weight[:, c * width : (c + 1) * width] for c in range(spans)]
        + [outer_weight],
        axis=0,
    )
    early = lax.all_gather(early_pack, "fsdp", axis=0, tiled=False)
    late = lax.all_gather(late_pack, "fsdp", axis=0, tiled=False)

    rows_all = to_whole_sequences(hidden)
    cot_all = to_whole_sequences(cotangent)
    segment_rows = lax.dynamic_slice_in_dim(segments, lax.axis_index("seq") * each, each, 0)

    def square(pack, index):
        return pack[:, index * part : (index + 1) * part].reshape(width, width)

    whole_query, whole_key, whole_value = (square(early, i) for i in range(3))
    flat_small = early[:, 3 * part :].reshape(owners, small_rows * width)
    vectors = []
    at = 0
    for size in small_sizes:
        vectors.append(flat_small[:, at : at + size].reshape(owners * size).astype(f32))
        at += size
    (
        query_shift,
        value_shift,
        output_shift,
        gain_one,
        shift_one,
        outer_shift,
        gain_two,
        shift_two,
        inner_shift,
    ) = vectors
    whole_output = square(late, 0)
    whole_inner = jnp.concatenate([square(late, 1 + c) for c in range(spans)], axis=1)
    whole_outer = late[:, (1 + spans) * part :].reshape(wide, width)

    length = rows_all.shape[1]
    rows = rows_all.reshape(each * length, width)
    grad_out = cot_all.reshape(each * length, width).astype(f32)

    query = (matmul(rows, whole_query) + query_shift).astype(bf16)
    keys = matmul(rows, whole_key).astype(bf16)
    values = (matmul(rows, whole_value) + value_shift).astype(bf16)
    cut = lambda array, i: array[i * length : (i + 1) * length]
    contexts, totals = [], []
    for i in range(each):
        piece, total = attention_forward(
            cut(query, i), cut(keys, i), cut(values, i), segment_rows[i], block_perm
        )
        contexts.append(piece)
        totals.append(total)
    context = jnp.concatenate(contexts, axis=0) if each > 1 else contexts[0]
    first = rows.astype(f32) + (matmul(context, whole_output) + output_shift)
    normed = norm_core(first, gain_one) + shift_one
    normed_low = normed.astype(bf16)
    inner = matmul(normed_low, whole_inner) + inner_shift
    active = exact_gelu(inner).astype(bf16)
    second = normed + (matmul(active, whole_outer) + outer_shift)
    result = norm_core(second, gain_two) + shift_two
    layer_out = to_token_shards(result.astype(bf16).reshape(each, length, width))

    _, second_back = jax.vjp(norm_core, second, gain_two)
    slope_second, grad_gain_two = second_back(grad_out)
    grad_shift_two = jnp.sum(grad_out, axis=0)
    slope_outer = slope_second.astype(bf16)
    grad_outer_shift = column_sum(slope_outer)
    grad_outer = transposed_times(active, slope_outer)
    _, gelu_back = jax.vjp(exact_gelu, inner)
    slope_inner = gelu_back(times_transposed(slope_outer, whole_outer))[0].astype(bf16)
    grad_inner_shift = column_sum(slope_inner)
    grad_inner = transposed_times(normed_low, slope_inner)
    late_grads = jnp.concatenate(
        [grad_inner[:, c * width : (c + 1) * width].astype(bf16).reshape(owners, part, width) for c in range(spans)]
        + [grad_outer.astype(bf16).reshape(owners, spans * part, width)],
        axis=1,
    )
    late_owned = lax.psum_scatter(late_grads, "fsdp", scatter_dimension=0, tiled=False)
    slope_normed = slope_second + times_transposed(slope_inner, whole_inner)
    _, first_back = jax.vjp(norm_core, first, gain_one)
    slope_first, grad_gain_one = first_back(slope_normed)
    grad_shift_one = jnp.sum(slope_normed, axis=0)
    slope_attn = slope_first.astype(bf16)
    grad_output_shift = column_sum(slope_attn)
    grad_output = transposed_times(context, slope_attn)
    slope_context = times_transposed(slope_attn, whole_output).astype(bf16)
    slopes = [
        attention_backward(
            cut(query, i),
            cut(keys, i),
            cut(values, i),
            cut(slope_context, i),
            segment_rows[i],
            block_perm,
            totals[i],
        )
        for i in range(each)
    ]
    slope_query, slope_keys, slope_values = (
        jnp.concatenate(parts, axis=0) if each > 1 else parts[0] for parts in zip(*slopes)
    )
    slope_rows = (
        slope_first
        + times_transposed(slope_query, whole_query)
        + times_transposed(slope_keys, whole_key)
        + times_transposed(slope_values, whole_value)
    )
    hidden_grad = to_token_shards(slope_rows.astype(bf16).reshape(each, length, width))
    grad_query = transposed_times(rows, slope_query)
    grad_query_shift = column_sum(slope_query)
    grad_key = transposed_times(rows, slope_keys)
    grad_value = transposed_times(rows, slope_values)
    grad_value_shift = column_sum(slope_values)
    small_grads = (
        grad_query_shift,
        grad_value_shift,
        grad_output_shift,
        grad_gain_one,
        grad_shift_one,
        grad_outer_shift,
        grad_gain_two,
        grad_shift_two,
        grad_inner_shift,
    )
    slab = lambda array: array.astype(bf16).reshape(owners, part, width)
    early_grads = jnp.concatenate(
        [slab(grad_query), slab(grad_key), slab(grad_value), slab(grad_output)]
        + [
            small_block(
                [piece.astype(bf16).reshape(owners, -1) for piece in small_grads], (owners,)
            )
        ],
        axis=1,
    )
    early_owned = lax.psum_scatter(early_grads, "fsdp", scatter_dimension=0, tiled=False)
    late_owned = sum_over_seq(late_owned).astype(f32)
    early_owned = sum_over_seq(early_owned).astype(f32)
    own = lambda pack, index: pack[index * part : (index + 1) * part]
    small_flat = early_owned[4 * part :].reshape(small_rows * width)
    got = []
    at = 0
    for size in small_sizes:
        got.append(small_flat[at : at + size])
        at += size
    (
        own_query_shift,
        own_value_shift,
        own_output_shift,
        own_gain_one,
        own_shift_one,
        own_outer_shift,
        own_gain_two,
        own_shift_two,
        own_inner_shift,
    ) = got
    own_inner = jnp.concatenate([own(late_owned, c) for c in range(spans)], axis=1)
    own_outer = late_owned[spans * part :]
    return (
        layer_out,
        hidden_grad,
        own(early_owned, 0),
        own_query_shift,
        own(early_owned, 1),
        own(early_owned, 2),
        own_value_shift,
        own(early_owned, 3),
        own_output_shift,
        own_gain_one,
        own_shift_one,
        own_inner,
        own_inner_shift,
        own_outer,
        own_outer_shift,
        own_gain_two,
        own_shift_two,
    )


def on_device(hidden, *rest):
    if hidden.shape[0] % lax.axis_size("seq") == 0:
        return on_device_whole(hidden, *rest)
    return on_device_general(hidden, *rest)


def solution(mesh):
    in_specs = (
        P("fsdp", "seq", None),
        P("fsdp", None),
        P(),
        P("fsdp", None),
        P("fsdp"),
        P("fsdp", None),
        P("fsdp", None),
        P("fsdp"),
        P("fsdp", None),
        P("fsdp"),
        P("fsdp"),
        P("fsdp"),
        P("fsdp", None),
        P("fsdp"),
        P("fsdp", None),
        P("fsdp"),
        P("fsdp"),
        P("fsdp"),
        P("fsdp", "seq", None),
    )
    out_specs = (
        P("fsdp", "seq", None),
        P("fsdp", "seq", None),
        P("fsdp", None),
        P("fsdp"),
        P("fsdp", None),
        P("fsdp", None),
        P("fsdp"),
        P("fsdp", None),
        P("fsdp"),
        P("fsdp"),
        P("fsdp"),
        P("fsdp", None),
        P("fsdp"),
        P("fsdp", None),
        P("fsdp"),
        P("fsdp"),
        P("fsdp"),
    )
    return jax.shard_map(
        on_device, mesh=mesh, in_specs=in_specs, out_specs=out_specs, check_vma=False
    )
```

```python
import functools

import jax
import jax.numpy as jnp
from jax import lax
from jax.experimental import pallas as pl
from jax.experimental.pallas import tpu as pltpu
from jax.sharding import PartitionSpec as P

H = 12
HD = 64


EPSILON = 1e-05


def shortened(array):
    return jax.tree.map(lambda a: a.astype(jnp.bfloat16) if a.dtype == jnp.float32 else a, array)


def norm_core(values, gain):
    average = jnp.mean(values, axis=-1, keepdims=True)
    centered = values - average
    spread = jnp.mean(centered * centered, axis=-1, keepdims=True)
    return centered * lax.rsqrt(spread + EPSILON) * gain


def exact_gelu(values):
    return jax.nn.gelu(values, approximate=False)


def matmul(left, right):
    return jnp.dot(left, right, preferred_element_type=jnp.float32)


def times_transposed(left, right):
    return lax.dot_general(
        left, right, (((1,), (1,)), ((), ())), preferred_element_type=jnp.float32
    )


def transposed_times(left, right):
    return lax.dot_general(
        left, right, (((0,), (0,)), ((), ())), preferred_element_type=jnp.float32
    )


def column_sum(values):
    return jnp.sum(values.astype(jnp.float32), axis=0)


def select_blocks(blocked, target):
    return jnp.take_along_axis(blocked, target[:, None, None, None], axis=1)[:, 0]


def block_scores(query_block, chosen_keys, query_segments, key_segments, scale):
    scores = (
        jnp.einsum("qhd,hkd->hqk", query_block, chosen_keys, preferred_element_type=jnp.float32)
        * scale
    )
    same_doc = query_segments[None, :, None] == key_segments[:, None, :]
    mirror = lax.broadcasted_iota(jnp.int32, scores.shape, 1) == lax.broadcasted_iota(
        jnp.int32, scores.shape, 2
    )
    return jnp.where(same_doc | mirror, scores, -1e30)


def split_layout(query_all, keys_all, values_all, segment_row, perm_local, head_dim):
    length, width = query_all.shape
    heads = width // head_dim
    block_count = perm_local.shape[1]
    block_rows = length // block_count
    shaped = (block_count, block_rows, heads, head_dim)
    query_split = query_all.reshape(shaped)
    keys_split = keys_all.reshape(shaped).transpose(2, 0, 1, 3)
    values_split = values_all.reshape(shaped).transpose(2, 0, 1, 3)
    segment_split = segment_row.reshape(block_count, block_rows)
    return (query_split, keys_split, values_split, segment_split, shaped)


def attend_forward(query_all, keys_all, values_all, segment_row, perm_local, head_dim):
    length, width = query_all.shape
    query_split, keys_split, values_split, segment_split, shaped = split_layout(
        query_all, keys_all, values_all, segment_row, perm_local, head_dim
    )
    scale = head_dim ** (-0.5)
    contexts = []
    log_totals = []
    for block in range(shaped[0]):
        target = perm_local[:, block]
        chosen_keys = select_blocks(keys_split, target)
        chosen_values = select_blocks(values_split, target)
        masked = block_scores(
            query_split[block], chosen_keys, segment_split[block], segment_split[target], scale
        )
        row_max = jnp.max(masked, axis=-1, keepdims=True)
        lifted = jnp.exp(masked - row_max)
        total = jnp.sum(lifted, axis=-1, keepdims=True)
        probs = (lifted / total).astype(jnp.bfloat16)
        piece = jnp.einsum("hqk,hkd->qhd", probs, chosen_values, preferred_element_type=jnp.float32)
        contexts.append(piece.astype(jnp.bfloat16))
        log_totals.append(row_max + jnp.log(total))
    return (jnp.concatenate(contexts, axis=0).reshape(length, width), jnp.stack(log_totals))


def attend_backward(
    query_all, keys_all, values_all, slope_all, segment_row, perm_local, log_totals, head_dim
):
    length, width = query_all.shape
    query_split, keys_split, values_split, segment_split, shaped = split_layout(
        query_all, keys_all, values_all, segment_row, perm_local, head_dim
    )
    block_count, block_rows, heads = (shaped[0], shaped[1], shaped[2])
    slope_split = slope_all.reshape(shaped)
    scale = head_dim ** (-0.5)
    key_slots = jnp.zeros((heads, block_count, block_rows, head_dim), jnp.float32)
    value_slots = jnp.zeros((heads, block_count, block_rows, head_dim), jnp.float32)
    block_ids = jnp.arange(block_count, dtype=jnp.int32)
    query_slopes = []
    for block in range(block_count):
        target = perm_local[:, block]
        chosen_keys = select_blocks(keys_split, target)
        chosen_values = select_blocks(values_split, target)
        masked = block_scores(
            query_split[block], chosen_keys, segment_split[block], segment_split[target], scale
        )
        probs = jnp.exp(masked - log_totals[block])
        slope_probs = jnp.einsum(
            "qhd,hkd->hqk", slope_split[block], chosen_values, preferred_element_type=jnp.float32
        )
        row_dot = jnp.sum(probs * slope_probs, axis=-1, keepdims=True)
        slope_scores = (probs * (slope_probs - row_dot)).astype(jnp.bfloat16)
        query_part = (
            jnp.einsum(
                "hqk,hkd->qhd", slope_scores, chosen_keys, preferred_element_type=jnp.float32
            )
            * scale
        )
        query_slopes.append(query_part.astype(jnp.bfloat16))
        key_part = (
            jnp.einsum(
                "hqk,qhd->hkd", slope_scores, query_split[block], preferred_element_type=jnp.float32
            )
            * scale
        )
        value_part = jnp.einsum(
            "hqk,qhd->hkd",
            probs.astype(jnp.bfloat16),
            slope_split[block],
            preferred_element_type=jnp.float32,
        )
        hit = (target[:, None] == block_ids[None, :])[:, :, None, None]
        key_slots = jnp.where(hit, key_part[:, None], key_slots)
        value_slots = jnp.where(hit, value_part[:, None], value_slots)
    slope_query = jnp.concatenate(query_slopes, axis=0).reshape(length, width)
    slope_keys = key_slots.transpose(1, 2, 0, 3).reshape(length, width).astype(jnp.bfloat16)
    slope_values = value_slots.transpose(1, 2, 0, 3).reshape(length, width).astype(jnp.bfloat16)
    return (slope_query, slope_keys, slope_values)


def on_device_general(
    hidden,
    segments,
    block_perm,
    query_weight,
    query_bias,
    key_weight,
    value_weight,
    value_bias,
    output_weight,
    output_bias,
    first_gain,
    first_shift,
    inner_weight,
    inner_bias,
    outer_weight,
    outer_bias,
    second_gain,
    second_shift,
    cotangent,
):
    micro = hidden.shape[0]
    heads_here = H // lax.axis_size("seq")
    perm_local = lax.dynamic_slice_in_dim(
        block_perm, lax.axis_index("seq") * heads_here, heads_here, 0
    )
    shards = (
        query_weight,
        query_bias,
        key_weight,
        value_weight,
        value_bias,
        output_weight,
        output_bias,
        first_gain,
        first_shift,
        inner_weight,
        inner_bias,
        outer_weight,
        outer_bias,
        second_gain,
        second_shift,
    )
    matrices = (
        query_weight,
        key_weight,
        value_weight,
        output_weight,
        inner_weight,
        outer_weight,
        first_gain,
        second_gain,
    )
    sums = tuple(
        (
            jnp.zeros((piece.shape[0] * lax.axis_size("fsdp"),) + piece.shape[1:], jnp.float32)
            for piece in shards
        )
    )
    f32 = jnp.float32
    bf16 = jnp.bfloat16

    def one_batch(index, carry):
        layer_out, hidden_grad, totals = carry
        rows = lax.dynamic_index_in_dim(hidden, index, 0, keepdims=False)
        segment_row = lax.dynamic_index_in_dim(segments, index, 0, keepdims=False)
        grad_out = lax.dynamic_index_in_dim(cotangent, index, 0, keepdims=False).astype(f32)
        ahead = (
            lax.all_gather(shards[0], "fsdp", axis=0, tiled=True),
            lax.all_gather(shards[1], "fsdp", axis=0, tiled=True),
            lax.all_gather(shards[2], "fsdp", axis=0, tiled=True),
            lax.all_gather(shards[3], "fsdp", axis=0, tiled=True),
            lax.all_gather(shards[4], "fsdp", axis=0, tiled=True),
            lax.all_gather(shards[5], "fsdp", axis=0, tiled=True),
            lax.all_gather(shards[6], "fsdp", axis=0, tiled=True),
            lax.all_gather(shards[7], "fsdp", axis=0, tiled=True),
            lax.all_gather(shards[8], "fsdp", axis=0, tiled=True),
            lax.all_gather(shards[9], "fsdp", axis=0, tiled=True),
            lax.all_gather(shards[10], "fsdp", axis=0, tiled=True),
            lax.all_gather(shards[11], "fsdp", axis=0, tiled=True),
            lax.all_gather(shards[12], "fsdp", axis=0, tiled=True),
            lax.all_gather(shards[13], "fsdp", axis=0, tiled=True),
            lax.all_gather(shards[14], "fsdp", axis=0, tiled=True),
        )
        (
            whole_query,
            query_shift,
            whole_key,
            whole_value,
            value_shift,
            whole_output,
            output_shift,
            gain_one,
            shift_one,
            whole_inner,
            inner_shift,
            whole_outer,
            outer_shift,
            gain_two,
            shift_two,
        ) = ahead
        query = (matmul(rows, whole_query) + query_shift.astype(f32)).astype(bf16)
        keys = matmul(rows, whole_key).astype(bf16)
        values = (matmul(rows, whole_value) + value_shift.astype(f32)).astype(bf16)
        query_all, keys_all, values_all = (
            lax.all_to_all(query, "seq", split_axis=1, concat_axis=0, tiled=True),
            lax.all_to_all(keys, "seq", split_axis=1, concat_axis=0, tiled=True),
            lax.all_to_all(values, "seq", split_axis=1, concat_axis=0, tiled=True),
        )
        context, log_totals = attend_forward(
            query_all, keys_all, values_all, segment_row, perm_local, HD
        )
        context_rows = lax.all_to_all(
            shortened(context), "seq", split_axis=0, concat_axis=1, tiled=True
        ).astype(context.dtype)
        first = rows.astype(f32) + (matmul(context_rows, whole_output) + output_shift.astype(f32))
        normed = norm_core(first, gain_one.astype(f32)) + shift_one.astype(f32)
        normed_low = normed.astype(bf16)
        inner = matmul(normed_low, whole_inner) + inner_shift.astype(f32)
        active = exact_gelu(inner).astype(bf16)
        second = normed + (matmul(active, whole_outer) + outer_shift.astype(f32))
        result = norm_core(second, gain_two.astype(f32)) + shift_two.astype(f32)
        behind = (
            lax.all_gather(matrices[0], "fsdp", axis=0, tiled=True),
            lax.all_gather(matrices[1], "fsdp", axis=0, tiled=True),
            lax.all_gather(matrices[2], "fsdp", axis=0, tiled=True),
            lax.all_gather(matrices[3], "fsdp", axis=0, tiled=True),
            lax.all_gather(matrices[4], "fsdp", axis=0, tiled=True),
            lax.all_gather(matrices[5], "fsdp", axis=0, tiled=True),
            lax.all_gather(matrices[6], "fsdp", axis=0, tiled=True),
            lax.all_gather(matrices[7], "fsdp", axis=0, tiled=True),
        )
        (
            back_query,
            back_key,
            back_value,
            back_output,
            back_inner,
            back_outer,
            back_gain_one,
            back_gain_two,
        ) = behind
        _, second_back = jax.vjp(norm_core, second, back_gain_two.astype(f32))
        slope_second, grad_gain_two = second_back(grad_out)
        grad_shift_two = jnp.sum(grad_out, axis=0)
        slope_outer = slope_second.astype(bf16)
        grad_outer_shift = column_sum(slope_outer)
        grad_outer = transposed_times(active, slope_outer)
        _, gelu_back = jax.vjp(exact_gelu, inner)
        slope_inner = gelu_back(times_transposed(slope_outer, back_outer))[0].astype(bf16)
        grad_inner_shift = column_sum(slope_inner)
        grad_inner = transposed_times(normed_low, slope_inner)
        slope_normed = slope_second + times_transposed(slope_inner, back_inner)
        _, first_back = jax.vjp(norm_core, first, back_gain_one.astype(f32))
        slope_first, grad_gain_one = first_back(slope_normed)
        grad_shift_one = jnp.sum(slope_normed, axis=0)
        slope_attn = slope_first.astype(bf16)
        grad_output_shift = column_sum(slope_attn)
        grad_output = transposed_times(context_rows, slope_attn)
        slope_context = times_transposed(slope_attn, back_output).astype(bf16)
        slope_context_all = lax.all_to_all(
            slope_context, "seq", split_axis=1, concat_axis=0, tiled=True
        )
        slope_query_all, slope_keys_all, slope_values_all = attend_backward(
            query_all,
            keys_all,
            values_all,
            slope_context_all,
            segment_row,
            perm_local,
            log_totals,
            HD,
        )
        slope_query, slope_keys, slope_values = (
            lax.all_to_all(
                shortened(slope_query_all), "seq", split_axis=0, concat_axis=1, tiled=True
            ).astype(slope_query_all.dtype),
            lax.all_to_all(slope_keys_all, "seq", split_axis=0, concat_axis=1, tiled=True),
            lax.all_to_all(slope_values_all, "seq", split_axis=0, concat_axis=1, tiled=True),
        )
        grad_query = transposed_times(rows, slope_query)
        grad_query_shift = column_sum(slope_query)
        grad_key = transposed_times(rows, slope_keys)
        grad_value = transposed_times(rows, slope_values)
        grad_value_shift = column_sum(slope_values)
        slope_rows = (
            slope_first
            + times_transposed(slope_query, back_query)
            + times_transposed(slope_keys, back_key)
            + times_transposed(slope_values, back_value)
        )
        grads = (
            grad_query,
            grad_query_shift,
            grad_key,
            grad_value,
            grad_value_shift,
            grad_output,
            grad_output_shift,
            grad_gain_one,
            grad_shift_one,
            grad_inner,
            grad_inner_shift,
            grad_outer,
            grad_outer_shift,
            grad_gain_two,
            grad_shift_two,
        )
        totals = jax.tree.map(lambda total, piece: total + piece, totals, grads)
        layer_out = lax.dynamic_update_index_in_dim(layer_out, result.astype(bf16), index, 0)
        hidden_grad = lax.dynamic_update_index_in_dim(
            hidden_grad, slope_rows.astype(bf16), index, 0
        )
        return (layer_out, hidden_grad, totals)

    start = (jnp.zeros(hidden.shape, bf16), jnp.zeros(hidden.shape, bf16), sums)
    layer_out, hidden_grad, sums = lax.fori_loop(0, micro, one_batch, start)
    owned = lax.psum_scatter(sums, "fsdp", scatter_dimension=0, tiled=True)
    sums = jax.tree.map(lambda part: part.astype(jnp.float32), lax.psum(shortened(owned), "seq"))
    return (layer_out, hidden_grad) + tuple(sums)


def dot(left, right, contract):
    return lax.dot_general(
        left, right, ((contract[:1], contract[1:]), ((), ())), preferred_element_type=jnp.float32
    )


def project_kernel(rows_ref, early_ref, small_ref, query_ref, keys_ref, values_ref):
    rows = rows_ref[...]
    part = part_of(early_ref)
    width = rows.shape[1]
    for index, (out_ref, bias) in enumerate(((query_ref, 0), (keys_ref, None), (values_ref, 1))):
        weight = early_ref[:, index * part : (index + 1) * part, :].reshape(width, width)
        product = dot(rows, weight, (1, 0))
        if bias is not None:
            product = product + small_ref[bias : bias + 1, :]
        out_ref[...] = product.astype(jnp.bfloat16)


def part_of(early_ref):
    return early_ref.shape[2] // early_ref.shape[0]


def project(rows, early, small):
    count, width = rows.shape
    tile = count // 2
    token = pl.BlockSpec((tile, width), lambda i: (i, 0))
    shape = jax.ShapeDtypeStruct((count, width), jnp.bfloat16)
    return pl.pallas_call(
        project_kernel,
        grid=(2,),
        in_specs=[
            token,
            pl.BlockSpec(early.shape, lambda i: (0, 0, 0), pipeline_mode=pl.Buffered(1)),
            pl.BlockSpec(small.shape, lambda i: (0, 0)),
        ],
        out_specs=[token, token, token],
        out_shape=[shape, shape, shape],
        name="project",
    )(rows, early, small)


def masked_probs(query, keys, same):
    scores = jnp.where(same, dot(keys, query, (1, 1)), -1e30)
    lifted = jnp.exp(scores - jnp.max(scores, axis=0, keepdims=True))
    return lifted * (1.0 / jnp.sum(lifted, axis=0, keepdims=True))


def visible(segment_row_ref, segment_column_ref, block, target, size):
    own = segment_row_ref[block : block + 1, :]
    other = segment_column_ref[pl.ds(pl.multiple_of(target * size, size), size), :]
    mirror = lax.broadcasted_iota(jnp.int32, (size, size), 0) == lax.broadcasted_iota(
        jnp.int32, (size, size), 1
    )
    return (own == other) | mirror


def attend_kernel(
    perm_ref, query_ref, keys_ref, values_ref, segment_row_ref, segment_column_ref, out_ref
):
    blocks, size = segment_row_ref.shape
    pair = query_ref.shape[1] // HD
    scale = HD**-0.5
    for j in range(pair):
        lanes = slice(j * HD, (j + 1) * HD)
        for block in range(blocks):
            target = perm_ref[pl.program_id(0) * pair + j, block]
            there = pl.ds(pl.multiple_of(target * size, size), size)
            here = slice(block * size, (block + 1) * size)
            same = visible(segment_row_ref, segment_column_ref, block, target, size)
            query = query_ref[here, lanes] * jnp.bfloat16(scale)
            probs = masked_probs(query, keys_ref[there, lanes], same).astype(jnp.bfloat16)
            piece = dot(values_ref[there, lanes], probs, (0, 0))
            out_ref[here, lanes] = piece.T.astype(jnp.bfloat16)


def attend_back_kernel(
    perm_ref,
    query_ref,
    keys_ref,
    values_ref,
    slope_ref,
    segment_row_ref,
    segment_column_ref,
    slope_query_ref,
    slope_keys_ref,
    slope_values_ref,
):
    blocks, size = segment_row_ref.shape
    pair = query_ref.shape[1] // HD
    scale = HD**-0.5
    bf16 = jnp.bfloat16
    for j in range(pair):
        lanes = slice(j * HD, (j + 1) * HD)
        for block in range(blocks):
            target = perm_ref[pl.program_id(0) * pair + j, block]
            there = pl.ds(pl.multiple_of(target * size, size), size)
            here = slice(block * size, (block + 1) * size)
            same = visible(segment_row_ref, segment_column_ref, block, target, size)
            query = query_ref[here, lanes] * bf16(scale)
            keys = keys_ref[there, lanes]
            slope = slope_ref[here, lanes]
            probs = masked_probs(query, keys, same)
            slope_probs = dot(values_ref[there, lanes], slope, (1, 1))
            row_dot = jnp.sum(probs * slope_probs, axis=0, keepdims=True)
            slope_scores = (probs * (slope_probs - row_dot)).astype(bf16)
            slope_query_ref[here, lanes] = (dot(keys, slope_scores, (0, 0)) * scale).T.astype(bf16)
            slope_keys_ref[there, lanes] = dot(slope_scores, query, (1, 0)).astype(bf16)
            slope_values_ref[there, lanes] = dot(probs.astype(bf16), slope, (1, 0)).astype(bf16)


def attend_call(kernel, arrays, segment_row, block_perm, outs, name):
    count, width = arrays[0].shape
    blocks = block_perm.shape[1]
    lanes = 2 * HD
    head = pl.BlockSpec((count, lanes), lambda i, perm: (0, i))
    row = segment_row.reshape(blocks, count // blocks)
    column = segment_row.reshape(count, 1)
    shape = jax.ShapeDtypeStruct((count, width), jnp.bfloat16)
    return pl.pallas_call(
        kernel,
        grid_spec=pltpu.PrefetchScalarGridSpec(
            num_scalar_prefetch=1,
            grid=(width // lanes,),
            in_specs=[head] * len(arrays)
            + [
                pl.BlockSpec(row.shape, lambda i, perm: (0, 0)),
                pl.BlockSpec(column.shape, lambda i, perm: (0, 0)),
            ],
            out_specs=[head] * outs,
        ),
        out_shape=[shape] * outs,
        name=name,
    )(block_perm, *arrays, row, column)


def normalize(values):
    average = jnp.mean(values, axis=-1, keepdims=True)
    centered = values - average
    spread = jnp.mean(centered * centered, axis=-1, keepdims=True)
    factor = lax.rsqrt(spread + EPSILON)
    return centered * factor, factor


def normalize_back(slope, unit, factor):
    return (
        slope
        - jnp.mean(slope, axis=-1, keepdims=True)
        - unit * jnp.mean(slope * unit, axis=-1, keepdims=True)
    ) * factor


def middle_kernel(
    tiles,
    halves,
    rows_ref,
    context_ref,
    cotangent_ref,
    late_ref,
    small_ref,
    inner_shift_ref,
    result_ref,
    slope_first_ref,
    slope_context_ref,
    grads_ref,
    small_grads_ref,
    inner_shift_grad_ref,
    active_ref,
    slope_inner_ref,
    slope_outer_ref,
    normed_ref,
    slope_attn_ref,
    context_all_ref,
    bend_ref,
):
    f32, bf16 = jnp.float32, jnp.bfloat16
    step = pl.program_id(0)
    owners, packed, width = late_ref.shape
    part = width // owners
    wide = active_ref.shape[1]
    spans = wide // width
    tile = rows_ref.shape[0]

    def inner_weight(c):
        return late_ref[:, (1 + c) * part : (2 + c) * part, :].reshape(width, width)

    def output_weight():
        return late_ref[:, :part, :].reshape(width, width)

    def outer_weight(c):
        few = owners // spans
        return late_ref[c * few : (c + 1) * few, (1 + spans) * part :, :].reshape(width, width)

    def total(values):
        return jnp.sum(values, axis=0, keepdims=True)

    @pl.when(step == 0)
    def _():
        small_grads_ref[...] = jnp.zeros_like(small_grads_ref)
        inner_shift_grad_ref[...] = jnp.zeros_like(inner_shift_grad_ref)

    @pl.when(step < tiles)
    def _():
        at = pl.ds(pl.multiple_of(step * tile, tile), tile)
        vector = lambda i: small_ref[i : i + 1, :]
        output_shift, gain_one, shift_one = vector(2), vector(3), vector(4)
        outer_shift, gain_two, shift_two = vector(5), vector(6), vector(7)
        context = context_ref[...]
        context_all_ref[at, :] = context
        attn = dot(context, output_weight(), (1, 0)) + output_shift
        unit_one, factor_one = normalize(rows_ref[...].astype(f32) + attn)
        normed = unit_one * gain_one + shift_one
        normed_low = normed.astype(bf16)
        normed_ref[at, :] = normed_low
        outer = jnp.zeros((tile, width), f32)
        for c in range(spans):
            span = slice(c * width, (c + 1) * width)
            inner = dot(normed_low, inner_weight(c), (1, 0)) + inner_shift_ref[:, span]
            phi = 0.5 * (1.0 + lax.erf(inner * (0.5**0.5)))
            density = jnp.exp(inner * inner * -0.5) * ((2.0 * jnp.pi) ** -0.5)
            bend_ref[:, span] = phi + inner * density
            active = (inner * phi).astype(bf16)
            active_ref[at, span] = active
            outer = outer + dot(active, outer_weight(c), (1, 0))
        second = normed + (outer + outer_shift)
        unit_two, factor_two = normalize(second)
        result_ref[...] = (unit_two * gain_two + shift_two).astype(bf16)
        cotangent = cotangent_ref[...].astype(f32)
        slope_second = normalize_back(cotangent * gain_two, unit_two, factor_two)
        slope_outer = slope_second.astype(bf16)
        slope_outer_ref[at, :] = slope_outer
        slope_normed = slope_second
        for c in range(spans):
            span = slice(c * width, (c + 1) * width)
            back = dot(slope_outer, outer_weight(c), (1, 1)) * bend_ref[:, span]
            slope_inner = back.astype(bf16)
            slope_inner_ref[at, span] = slope_inner
            inner_shift_grad_ref[:, span] += total(slope_inner.astype(f32))
            slope_normed = slope_normed + dot(slope_inner, inner_weight(c), (1, 1))
        slope_first = normalize_back(slope_normed * gain_one, unit_one, factor_one)
        slope_first_ref[...] = slope_first
        slope_attn = slope_first.astype(bf16)
        slope_attn_ref[at, :] = slope_attn
        slope_context_ref[...] = dot(slope_attn, output_weight(), (1, 1)).astype(bf16)
        small_grads_ref[2:3, :] += total(slope_attn.astype(f32))
        small_grads_ref[3:4, :] += total(slope_normed * unit_one)
        small_grads_ref[4:5, :] += total(slope_normed)
        small_grads_ref[5:6, :] += total(slope_outer.astype(f32))
        small_grads_ref[6:7, :] += total(cotangent * unit_two)
        small_grads_ref[7:8, :] += total(cotangent)

    few = owners // halves
    for half in range(halves):

        @pl.when(step == tiles + half)
        def _():
            mine = slice(half * few * part, (half + 1) * few * part)

            def put(first, count, left, right):
                product = dot(left, right, (0, 0)).astype(bf16)
                grads_ref[:, first : first + count, :] = product.reshape(few, count, width)

            put(0, part, context_all_ref[:, mine], slope_attn_ref[...])
            for c in range(spans):
                span = slice(c * width, (c + 1) * width)
                put((1 + c) * part, part, normed_ref[:, mine], slope_inner_ref[:, span])
            deep = slice(half * few * part * spans, (half + 1) * few * part * spans)
            put((1 + spans) * part, spans * part, active_ref[:, deep], slope_outer_ref[...])


def middle(rows, context, cotangent, late, small, inner_shift):
    count, width = rows.shape
    wide = inner_shift.shape[1]
    owners, packed, _ = late.shape
    tiles, halves = 4, 2
    tile = count // tiles
    f32, bf16 = jnp.float32, jnp.bfloat16
    token = pl.BlockSpec((tile, width), lambda i: (jnp.minimum(i, tiles - 1), 0))
    fixed = lambda shape: pl.BlockSpec(
        shape, lambda i: (0,) * len(shape), pipeline_mode=pl.Buffered(1)
    )
    whole = lambda shape: pl.BlockSpec(shape, lambda i: (0,) * len(shape))
    return pl.pallas_call(
        functools.partial(middle_kernel, tiles, halves),
        grid=(tiles + halves,),
        in_specs=[
            token,
            token,
            token,
            fixed(late.shape),
            fixed(small.shape),
            fixed(inner_shift.shape),
        ],
        out_specs=[
            token,
            token,
            token,
            pl.BlockSpec(
                (owners // halves, packed, width), lambda i: (jnp.maximum(i - tiles, 0), 0, 0)
            ),
            whole((8, width)),
            whole((1, wide)),
        ],
        out_shape=[
            jax.ShapeDtypeStruct((count, width), bf16),
            jax.ShapeDtypeStruct((count, width), f32),
            jax.ShapeDtypeStruct((count, width), bf16),
            jax.ShapeDtypeStruct(late.shape, bf16),
            jax.ShapeDtypeStruct((8, width), f32),
            jax.ShapeDtypeStruct((1, wide), f32),
        ],
        scratch_shapes=[
            pltpu.VMEM((count, wide), bf16),
            pltpu.VMEM((count, wide), bf16),
            pltpu.VMEM((count, width), bf16),
            pltpu.VMEM((count, width), bf16),
            pltpu.VMEM((count, width), bf16),
            pltpu.VMEM((count, width), bf16),
            pltpu.VMEM((tile, wide), f32),
        ],
        name="middle",
        compiler_params=pltpu.CompilerParams(vmem_limit_bytes=60 << 20),
    )(rows, context, cotangent, late, small, inner_shift)


def last_kernel(
    rows_ref,
    slope_query_ref,
    slope_keys_ref,
    slope_values_ref,
    slope_first_ref,
    early_ref,
    hidden_grad_ref,
    grads_ref,
    shift_grads_ref,
):
    half = pl.program_id(0)
    f32, bf16 = jnp.float32, jnp.bfloat16
    few = grads_ref.shape[0]
    width = rows_ref.shape[1]
    part = part_of(early_ref)
    tile = hidden_grad_ref.shape[0]
    at = pl.ds(pl.multiple_of(half * tile, tile), tile)
    mine = rows_ref[:, pl.ds(pl.multiple_of(half * few * part, few * part), few * part)]
    grad = slope_first_ref[...]
    for index, ref in enumerate((slope_query_ref, slope_keys_ref, slope_values_ref)):
        weight = early_ref[:, index * part : (index + 1) * part, :].reshape(width, width)
        grad = grad + dot(ref[at, :], weight, (1, 1))
        grads_ref[:, index * part : (index + 1) * part, :] = (
            dot(mine, ref[...], (0, 0)).astype(bf16).reshape(few, part, width)
        )
    hidden_grad_ref[...] = grad.astype(bf16)
    grads_ref[:, 3 * part :, :] = jnp.zeros_like(grads_ref[:, 3 * part :, :])

    @pl.when(half == 0)
    def _():
        shift_grads_ref[0:1, :] = jnp.sum(slope_query_ref[...].astype(f32), axis=0, keepdims=True)
        shift_grads_ref[1:2, :] = jnp.sum(slope_values_ref[...].astype(f32), axis=0, keepdims=True)


def last(rows, slope_query, slope_keys, slope_values, slope_first, early):
    count, width = rows.shape
    owners = early.shape[0]
    f32, bf16 = jnp.float32, jnp.bfloat16
    full = pl.BlockSpec((count, width), lambda i: (0, 0), pipeline_mode=pl.Buffered(1))
    token = pl.BlockSpec((count // 2, width), lambda i: (i, 0))
    return pl.pallas_call(
        last_kernel,
        grid=(2,),
        in_specs=[full] * 4
        + [
            token,
            pl.BlockSpec(early.shape, lambda i: (0, 0, 0), pipeline_mode=pl.Buffered(1)),
        ],
        out_specs=[
            token,
            pl.BlockSpec((owners // 2,) + early.shape[1:], lambda i: (i, 0, 0)),
            pl.BlockSpec((2, width), lambda i: (0, 0)),
        ],
        out_shape=[
            jax.ShapeDtypeStruct((count, width), bf16),
            jax.ShapeDtypeStruct(early.shape, bf16),
            jax.ShapeDtypeStruct((2, width), f32),
        ],
        name="last",
    )(rows, slope_query, slope_keys, slope_values, slope_first, early)


def to_whole_sequences(array):
    return lax.all_to_all(array, "seq", split_axis=0, concat_axis=1, tiled=True)


def to_token_shards(array):
    return lax.all_to_all(array, "seq", split_axis=1, concat_axis=0, tiled=True)


def sum_over_seq(array):
    if lax.axis_size("seq") == 2:
        return array + lax.ppermute(array, "seq", [(0, 1), (1, 0)])
    return lax.psum(array, "seq")


def on_device_whole(
    hidden,
    segments,
    block_perm,
    query_weight,
    query_bias,
    key_weight,
    value_weight,
    value_bias,
    output_weight,
    output_bias,
    first_gain,
    first_shift,
    inner_weight,
    inner_bias,
    outer_weight,
    outer_bias,
    second_gain,
    second_shift,
    cotangent,
):
    f32 = jnp.float32
    bf16 = jnp.bfloat16
    micro = hidden.shape[0]
    seqs = lax.axis_size("seq")
    owners = lax.axis_size("fsdp")
    each = micro // seqs
    part, width = query_weight.shape
    wide = inner_weight.shape[1]
    spans = wide // width
    small = (
        query_bias,
        value_bias,
        output_bias,
        first_gain,
        first_shift,
        outer_bias,
        second_gain,
        second_shift,
        inner_bias,
    )
    small_sizes = [piece.shape[0] for piece in small]
    small_count = sum(small_sizes)
    small_rows = -(-small_count // (16 * width)) * 16

    def small_block(pieces, lead):
        flat = jnp.concatenate(pieces, axis=-1)
        flat = jnp.pad(flat, [(0, 0)] * len(lead) + [(0, small_rows * width - small_count)])
        return flat.reshape(lead + (small_rows, width))

    early_pack = jnp.concatenate(
        [query_weight, key_weight, value_weight, small_block(small, ())], axis=0
    )
    late_pack = jnp.concatenate(
        [output_weight]
        + [inner_weight[:, c * width : (c + 1) * width] for c in range(spans)]
        + [outer_weight],
        axis=0,
    )
    early = lax.all_gather(early_pack, "fsdp", axis=0, tiled=False)
    late = lax.all_gather(late_pack, "fsdp", axis=0, tiled=False)

    rows_all = to_whole_sequences(hidden)
    cot_all = to_whole_sequences(cotangent)
    segment_rows = lax.dynamic_slice_in_dim(segments, lax.axis_index("seq") * each, each, 0)

    flat_small = early[:, 3 * part :].reshape(owners, small_rows * width)
    vectors = []
    at = 0
    for size in small_sizes:
        vectors.append(flat_small[:, at : at + size].reshape(1, owners * size).astype(f32))
        at += size
    small_vectors = jnp.concatenate(vectors[:-1], axis=0)

    length = rows_all.shape[1]
    rows = rows_all.reshape(length, width)
    segment_row = segment_rows.reshape(length)
    query, keys, values = project(rows, early, small_vectors)
    (context,) = attend_call(
        attend_kernel, (query, keys, values), segment_row, block_perm, 1, "attend"
    )
    result, slope_first, slope_context, late_grads, small_grads, inner_shift_grad = middle(
        rows, context, cot_all.reshape(length, width), late, small_vectors, vectors[-1]
    )
    layer_out = to_token_shards(result.reshape(each, length, width))
    late_owned = lax.psum_scatter(late_grads, "fsdp", scatter_dimension=0, tiled=False)
    slope_query, slope_keys, slope_values = attend_call(
        attend_back_kernel,
        (query, keys, values, slope_context),
        segment_row,
        block_perm,
        3,
        "attend_back",
    )
    slope_rows, early_grads, shift_grads = last(
        rows, slope_query, slope_keys, slope_values, slope_first, early
    )
    hidden_grad = to_token_shards(slope_rows.reshape(each, length, width))
    small_grads = jnp.concatenate(
        [
            jnp.concatenate([shift_grads, small_grads[2:]], axis=0)
            .reshape(-1, owners, part)
            .swapaxes(0, 1)
            .reshape(owners, -1),
            inner_shift_grad.reshape(owners, -1),
        ],
        axis=1,
    ).astype(bf16)
    early_grads = lax.dynamic_update_slice(
        early_grads, small_block([small_grads], (owners,)), (0, 3 * part, 0)
    )
    early_grads, late_owned = lax.optimization_barrier((early_grads, late_owned))
    early_owned = lax.psum_scatter(early_grads, "fsdp", scatter_dimension=0, tiled=False)
    late_owned = sum_over_seq(late_owned).astype(f32)
    early_owned = sum_over_seq(early_owned).astype(f32)
    own = lambda pack, index: pack[index * part : (index + 1) * part]
    small_flat = early_owned[3 * part :].reshape(small_rows * width)
    got = []
    at = 0
    for size in small_sizes:
        got.append(small_flat[at : at + size])
        at += size
    (
        own_query_shift,
        own_value_shift,
        own_output_shift,
        own_gain_one,
        own_shift_one,
        own_outer_shift,
        own_gain_two,
        own_shift_two,
        own_inner_shift,
    ) = got
    own_inner = jnp.concatenate([own(late_owned, 1 + c) for c in range(spans)], axis=1)
    own_outer = late_owned[(1 + spans) * part :]
    return (
        layer_out,
        hidden_grad,
        own(early_owned, 0),
        own_query_shift,
        own(early_owned, 1),
        own(early_owned, 2),
        own_value_shift,
        own(late_owned, 0),
        own_output_shift,
        own_gain_one,
        own_shift_one,
        own_inner,
        own_inner_shift,
        own_outer,
        own_outer_shift,
        own_gain_two,
        own_shift_two,
    )


def on_device(hidden, *rest):
    if hidden.shape[0] == lax.axis_size("seq"):
        return on_device_whole(hidden, *rest)
    return on_device_general(hidden, *rest)


def solution(mesh):
    in_specs = (
        P("fsdp", "seq", None),
        P("fsdp", None),
        P(),
        P("fsdp", None),
        P("fsdp"),
        P("fsdp", None),
        P("fsdp", None),
        P("fsdp"),
        P("fsdp", None),
        P("fsdp"),
        P("fsdp"),
        P("fsdp"),
        P("fsdp", None),
        P("fsdp"),
        P("fsdp", None),
        P("fsdp"),
        P("fsdp"),
        P("fsdp"),
        P("fsdp", "seq", None),
    )
    out_specs = (
        P("fsdp", "seq", None),
        P("fsdp", "seq", None),
        P("fsdp", None),
        P("fsdp"),
        P("fsdp", None),
        P("fsdp", None),
        P("fsdp"),
        P("fsdp", None),
        P("fsdp"),
        P("fsdp"),
        P("fsdp"),
        P("fsdp", None),
        P("fsdp"),
        P("fsdp", None),
        P("fsdp"),
        P("fsdp"),
        P("fsdp"),
    )
    return jax.shard_map(
        on_device, mesh=mesh, in_specs=in_specs, out_specs=out_specs, check_vma=False
    )
```
